32 devices in a mesh: row: 8 (over z, x), col: 4 (over y, core).
Axes of the slice: x: 2, y: 2, z: 4, core: 2. Of those that a mesh axis runs over, the one named last changes fastest.
Arguments:
- layer_input: bfloat16 [16384, 960], P(('row', 'col')), may hold values from -6 to 6
- norm1_gain: float32 [960], replicated, may hold values from 0.5 to 1.5
- w_qkv: bfloat16 [960, 1600], P('row', 'col'), may hold values from -0.1875 to 0.1875
- w_out: bfloat16 [960, 960], P('row', 'col'), may hold values from -1.5 to 1.5
- norm2_gain: float32 [960], replicated, may hold values from 0.5 to 1.5
- w_gate: bfloat16 [960, 2560], P('row', 'col'), may hold values from -0.1875 to 0.1875
- w_up: bfloat16 [960, 2560], P('row', 'col'), may hold values from -0.1875 to 0.1875
- w_down: bfloat16 [960, 2560], P('row', 'col'), may hold values from -0.15625 to 0.15625
- out_cotangent: bfloat16 [16384, 960], P(('row', 'col')), may hold values from -6 to 6
- seq_lengths: int32 [8, 3], P('row'), may hold values from 1 to 1024, 2048 in all within a row
- position_ids: int32 [16384], P(('row', 'col')), may hold values from 0 to 4094, as said below
- deal_rows: int32 [32, 8], P(('row', 'col')), may hold values from 0 to 7, each once within a row
Outputs:
- layer_output: bfloat16 [16384, 960], P(('row', 'col'))
- grad_input: bfloat16 [16384, 960], P(('row', 'col'))
- grad_norm1: float32 [960], replicated
- grad_qkv: float32 [960, 1600], P('row', 'col')
- grad_out: float32 [960, 960], P('row', 'col')
- grad_norm2: float32 [960], replicated
- grad_gate: float32 [960, 2560], P('row', 'col')
- grad_up: float32 [960, 2560], P('row', 'col')
- grad_down: float32 [960, 2560], P('row', 'col')
The draws below stay inside these ranges and needn't reach their ends.
Inputs may be any that keep to these rules, and one draw needn't show every extreme that they name: Each row of seq_lengths gives the lengths of the 3 sequences packed in order into one row group of 2048 dealt rows; each row sums to 2048, and its largest entry is exactly 1024. `position_ids`: within each aligned group of 2048 dealt rows the ids start at 0 and rise by 1 or 2 from one row to the next; in some group they rise by 2 at every row. `deal_rows`: each row is a permutation of the 8 row groups.
All inputs are finite; a program needn't handle non-finite values.
Results may differ from the reference program's by a relative error of at most 0.015.
Values may be sent and summed in bfloat16 or wider, within the bound.
A program may use at most 128 MiB of HBM per device.

```python
import math
import jax
import jax.numpy as jnp
import numpy as np
from jax import lax

D = 960
QUERY_HEADS = 15
KEY_VALUE_HEADS = 5
HEAD_DIMENSION = 64
FF = 2560
TOK_DEV = 512
SEQ_GRP = 3
QUERY_FEATURES = 960
KEY_FEATURES = 320
QKV = 1600
TOK_ROW = 2048
TOKENS = 16384
LMAX = 1024
N_ROW = 8
N_COL = 4


def draw_position_ids(key, part):
    group_count = TOKENS // TOK_ROW
    step_key = jax.random.fold_in(key, 11)
    pick_key = jax.random.fold_in(key, 23)
    increments = jax.random.randint(step_key, (group_count, TOK_ROW), 1, 3)
    chosen = jax.random.randint(pick_key, (), 0, group_count)
    group_index = jnp.arange(group_count, dtype=jnp.int32)[:, None]
    increments = jnp.where(group_index == chosen, 2, increments)
    places = jnp.cumsum(increments, axis=1) - increments
    return places.reshape(TOKENS).astype(jnp.int32)


def steps_of(rng, shape, cuts, least, largest):
    level = 1.0
    for dim, parts in cuts:
        draws = jax.random.uniform(jax.random.fold_in(jax.random.fold_in(rng, 6), dim), (parts,), jnp.float32, least / len(cuts), largest / len(cuts))
        level = level * jnp.repeat(jnp.exp(draws), shape[dim] // parts).reshape((-1,) + (1,) * (len(shape) - 1 - dim))
    return level


def length_profile(number_of, total, limit, skew):
    portions = [(1 << 20) // math.isqrt(standing ** skew) + 1 for standing in range(2, number_of + 1)]
    surplus, given = total - limit - (number_of - 1), [1] * (number_of - 1)
    while surplus > 0:
        free = [i for i in range(number_of - 1) if given[i] < limit]
        mass, budget = sum([portions[i] for i in free]), surplus
        for i in free:
            addition = min(limit - given[i], max(1, budget * portions[i] // mass), surplus)
            given[i] = given[i] + addition
            surplus = surplus - addition
    return np.array([limit] + given)


def uneven_parts(own_key, count, total, reach, lean):
    if count == 2:
        one = jax.random.randint(own_key, (), max(1, total - reach), min(reach, total - 1) + 1)
        return jnp.stack([one, total - one])
    lengths = jnp.asarray(length_profile(count, total, reach, lean), jnp.int32)
    pairs = (count - 1) // 2
    source_of, taker = lengths[1:1 + 2 * pairs:2], lengths[2:2 + 2 * pairs:2]
    margin = jnp.minimum(source_of - 1, reach - taker)
    passed = jax.random.randint(jax.random.fold_in(own_key, 1), (pairs,), 0, 1 << 20) % (margin + 1)
    lengths = lengths.at[1:1 + 2 * pairs:2].set(source_of - passed).at[2:2 + 2 * pairs:2].set(taker + passed)
    return lengths[jax.random.permutation(jax.random.fold_in(own_key, 2), count)]


def gaussian(stream_key, shape, width, bound, cuts=(), kind=jnp.bfloat16):
    gain = steps_of(stream_key, shape, cuts, -0.22, 0.18) if cuts else 1.0
    array = jax.random.normal(stream_key, shape, jnp.float32) * width * gain
    return jnp.minimum(jnp.maximum(array, -bound), bound).astype(kind)


def setup_inputs(seed: int = 0) -> dict:
    splits = jax.random.split(jax.random.key(seed), 13)
    layer_input = gaussian(splits[0], (TOKENS, D), 1.0, 6.0, ((0, 32),))
    norm1_gain = jnp.clip(1.0 + 0.1 * jax.random.normal(splits[1], (D,), jnp.float32), 0.5, 1.5)
    w_qkv = gaussian(splits[2], (D, QKV), D ** -0.5, 0.1875, ((0, 8), (1, 4)))
    w_out = gaussian(splits[3], (D, QUERY_FEATURES), (max(QUERY_FEATURES // 64, 1)) ** -0.5, 1.5, ((0, 8), (1, 4)))
    norm2_gain = jnp.clip(1.0 + 0.1 * jax.random.normal(splits[4], (D,), jnp.float32), 0.5, 1.5)
    w_gate = gaussian(splits[5], (D, FF), D ** -0.5, 0.1875, ((0, 8), (1, 4)))
    w_up = gaussian(splits[6], (D, FF), D ** -0.5, 0.1875, ((0, 8), (1, 4)))
    w_down = gaussian(splits[7], (D, FF), (FF // 2) ** -0.5, 0.15625, ((0, 8), (1, 4)))
    out_cotangent = gaussian(splits[8], (TOKENS, D), 1.0, 6.0, ((0, 32),))
    seq_lengths = jax.vmap(lambda own: uneven_parts(own, SEQ_GRP, TOK_ROW, LMAX, 2))(jax.random.split(splits[9], N_ROW)).reshape((N_ROW, SEQ_GRP)).astype(jnp.int32)
    position_ids = draw_position_ids(jax.random.fold_in(splits[12], 71), 0)
    deal_rows = jax.vmap(lambda own: jax.random.permutation(own, N_ROW))(jax.random.split(splits[11], (N_ROW * N_COL))).reshape((N_ROW * N_COL, N_ROW)).astype(jnp.int32)
    return dict(layer_input=layer_input, norm1_gain=norm1_gain, w_qkv=w_qkv, w_out=w_out, norm2_gain=norm2_gain, w_gate=w_gate, w_up=w_up, w_down=w_down, out_cotangent=out_cotangent, seq_lengths=seq_lengths, position_ids=position_ids, deal_rows=deal_rows)


EPS = 1e-05
NEG_FILL = -1e+30
THETA = 10000.0

@jax.custom_vjp
def lower_precision(v):
    return lax.optimization_barrier(v.astype(jnp.bfloat16)).astype(jnp.float32)

@jax.custom_vjp
def low_back(v):
    return v

def low_keep(v):
    return (lower_precision(v), None)

def low_pass(kept, grad):
    return (grad,)

def back_keep(v):
    return (v, None)

def back_low(kept, grad):
    return (lower_precision(grad),)
lower_precision.defvjp(low_keep, low_pass)
low_back.defvjp(back_keep, back_low)

def matmul(left_mat, right_mat):
    return jnp.dot(left_mat, right_mat, precision=lax.Precision.HIGHEST, preferred_element_type=jnp.float32)

def rms_scale(values):
    return lax.rsqrt(lax.optimization_barrier(jnp.mean(values * values, axis=1, keepdims=True)) + EPS)

def rope_tables(position, head_size):
    half_size = head_size // 2
    inverse = jnp.exp(jnp.arange(half_size, dtype=jnp.float32) * (-2.0 * math.log(THETA) / head_size))
    angles = position.astype(jnp.float32)[:, None] * inverse[None, :]
    return (jnp.cos(angles), jnp.sin(angles))

def apply_rotation(values, cosine_table, sine_table, head_count):
    pieces = values.reshape(values.shape[0], head_count, -1)
    half_size = pieces.shape[2] // 2
    first_half = pieces[:, :, :half_size]
    second_half = pieces[:, :, half_size:]
    cos_wide = cosine_table[:, None, :]
    sin_wide = sine_table[:, None, :]
    turned = jnp.concatenate([first_half * cos_wide - second_half * sin_wide, second_half * cos_wide + first_half * sin_wide], axis=2)
    return turned.reshape(values.shape)

def attention(query_r, key_repeated, value_full, allowed):
    row_counts = query_r.shape[0]
    query_heads = query_r.reshape(row_counts, QUERY_HEADS, HEAD_DIMENSION).transpose(1, 0, 2)
    heads_of_key = key_repeated.reshape(row_counts, KEY_VALUE_HEADS, HEAD_DIMENSION).transpose(1, 0, 2)
    heads_of_value = value_full.reshape(row_counts, KEY_VALUE_HEADS, HEAD_DIMENSION).transpose(1, 0, 2)
    heads_per_group = QUERY_HEADS // KEY_VALUE_HEADS
    factor = 1.0 / math.sqrt(HEAD_DIMENSION)

    def one_head(head_index):
        query_rows = lax.dynamic_index_in_dim(query_heads, head_index, 0, keepdims=False)
        key_rows = lax.dynamic_index_in_dim(heads_of_key, head_index // heads_per_group, 0, keepdims=False)
        value_rows = lax.dynamic_index_in_dim(heads_of_value, head_index // heads_per_group, 0, keepdims=False)
        scores = low_back(matmul(query_rows, key_rows.T) * factor)
        scores = jnp.where(allowed, scores, NEG_FILL)
        row_max = lax.optimization_barrier(jnp.max(scores, axis=1, keepdims=True))
        weights = jnp.exp(scores - row_max)
        probs = weights / lax.optimization_barrier(jnp.sum(weights, axis=1, keepdims=True))
        return matmul(lower_precision(probs), value_rows)
    head_outputs = lax.map(jax.checkpoint(one_head), jnp.arange(QUERY_HEADS, dtype=jnp.int32))
    return head_outputs.transpose(1, 0, 2).reshape(row_counts, QUERY_FEATURES)

def group_layer(group_input, group_ids, group_lengths, params):
    gain_one, qkv_weight, out_weight, gain_two, gate_weight, up_weight, down_weight = params
    row_counts = group_input.shape[0]
    row_ids = jnp.arange(row_counts, dtype=jnp.int32)
    bounds = jnp.cumsum(group_lengths)
    seg_ids = lax.optimization_barrier(jnp.sum((row_ids[:, None] >= bounds[None, :]).astype(jnp.int32), axis=1))
    allowed = (seg_ids[:, None] == seg_ids[None, :]) & (row_ids[None, :] <= row_ids[:, None])
    normed_one = group_input * rms_scale(group_input)
    xn_one = lower_precision(normed_one * gain_one)
    query_key_value_rows = lower_precision(low_back(matmul(xn_one, qkv_weight)))
    cosine_table, sine_table = rope_tables(group_ids, HEAD_DIMENSION)
    query_r = lower_precision(apply_rotation(query_key_value_rows[:, :QUERY_FEATURES], cosine_table, sine_table, QUERY_HEADS))
    key_repeated = lower_precision(apply_rotation(query_key_value_rows[:, QUERY_FEATURES:QUERY_FEATURES + KEY_FEATURES], cosine_table, sine_table, KEY_VALUE_HEADS))
    value_full = query_key_value_rows[:, QUERY_FEATURES + KEY_FEATURES:]
    attn_own = lower_precision(low_back(attention(query_r, key_repeated, value_full, allowed)))
    residual = group_input + low_back(matmul(attn_own, out_weight.T))
    normed_two = residual * rms_scale(residual)
    xn_two = lower_precision(normed_two * gain_two)
    gate_pre = low_back(matmul(xn_two, gate_weight))
    up_pre = low_back(matmul(xn_two, up_weight))
    hidden = lower_precision(jax.nn.silu(gate_pre) * up_pre)
    return residual + low_back(matmul(hidden, down_weight.T))

def dealt_places(deal_rows):
    devices = N_ROW * N_COL
    device_ids = jnp.arange(devices, dtype=jnp.int32)
    block_rows = TOK_DEV // N_ROW
    source_row = device_ids // N_COL
    source_col = device_ids % N_COL
    starts = (deal_rows * N_COL + source_col[:, None]) * TOK_DEV + source_row[:, None] * block_rows
    places = starts[:, :, None] + jnp.arange(block_rows, dtype=jnp.int32)[None, None, :]
    return places.reshape(devices * TOK_DEV).astype(jnp.int32)

def reference(layer_input, norm1_gain, w_qkv, w_out, norm2_gain, w_gate, w_up, w_down, out_cotangent, seq_lengths, position_ids, deal_rows):
    places = dealt_places(deal_rows)
    sources = jnp.argsort(places).astype(jnp.int32)
    dealt_input = layer_input[sources].astype(jnp.float32).reshape(N_ROW, TOK_ROW, D)
    dealt_cot = out_cotangent[sources].astype(jnp.float32).reshape(N_ROW, TOK_ROW, D)
    group_pos = position_ids.reshape(N_ROW, TOK_ROW)
    params = (norm1_gain.astype(jnp.float32), w_qkv.astype(jnp.float32), w_out.astype(jnp.float32), norm2_gain.astype(jnp.float32), w_gate.astype(jnp.float32), w_up.astype(jnp.float32), w_down.astype(jnp.float32))

    def one_group(totals, element):
        group_input, group_cot, group_ids, group_lengths = element

        def layer_fn(values, weights):
            return group_layer(values, group_ids, group_lengths, weights)
        group_out, pullback = jax.vjp(layer_fn, group_input, params)
        input_grad, weight_grads = pullback(group_cot)
        totals = tuple((total_now + grad_now for total_now, grad_now in zip(totals, weight_grads)))
        return (totals, (group_out.astype(jnp.bfloat16), input_grad.astype(jnp.bfloat16)))
    zeros = tuple((jnp.zeros(weight_now.shape, jnp.float32) for weight_now in params))
    totals, (outputs, input_grads) = lax.scan(one_group, zeros, (dealt_input, dealt_cot, group_pos, seq_lengths))
    layer_output = outputs.reshape(TOKENS, D)[places]
    grad_input = input_grads.reshape(TOKENS, D)[places]
    return (layer_output, grad_input, totals[0], totals[1], totals[2], totals[3], totals[4], totals[5], totals[6])
```

```python
import math
import functools

import jax
import jax.numpy as jnp
from jax import lax
from jax.experimental import pallas as pl
from jax.experimental.pallas import tpu as pltpu
from jax.sharding import PartitionSpec as P

QUERY_HEADS = 15
KEY_VALUE_HEADS = 5
HEADS_PER_GROUP = 3
HEAD_DIMENSION = 64
QUERY_FEATURES = 960
KEY_FEATURES = 320
LONGEST = 1024

EPS = 1e-05
NEG_FILL = -1e30
THETA = 10000.0
LANES = 128
TILE = 256
VMEM_BYTES = 60 << 20

F32 = jnp.float32
BF16 = jnp.bfloat16


def nn(left_mat, right_mat):
    return jnp.dot(left_mat, right_mat, preferred_element_type=F32)


def nt(left_mat, right_mat):
    return lax.dot_general(
        left_mat, right_mat, (((1,), (1,)), ((), ())), preferred_element_type=F32
    )


def lane_ids(rows):
    return lax.broadcasted_iota(jnp.int32, (rows, LANES), 1)


def keep_low(values):
    return jnp.where(lane_ids(values.shape[0]) < HEAD_DIMENSION, values, 0.0)


def keep_high(values):
    return jnp.where(lane_ids(values.shape[0]) >= HEAD_DIMENSION, values, 0.0)


def swap_halves(values):
    return pltpu.roll(values, HEAD_DIMENSION, 1)


def turn(values, cosine, sine):
    ids = lane_ids(values.shape[0])
    first = lax.rem(ids, HEAD_DIMENSION) < HEAD_DIMENSION // 2
    ahead = pltpu.roll(values, LANES - HEAD_DIMENSION // 2, 1)
    behind = pltpu.roll(values, HEAD_DIMENSION // 2, 1)
    return values * cosine + jnp.where(first, ahead, behind) * sine


def rms_scale(values):
    return lax.rsqrt(jnp.mean(values * values, axis=1, keepdims=True) + EPS)


def full_spec(shape):
    return pl.BlockSpec(shape, lambda *_: (0,) * len(shape))


def project_kernel(x_ref, gain_ref, w_ref, cos_ref, sin_ref, q_ref, kv_ref, rows_scr):
    own_rows = x_ref.shape[0]
    width = w_ref.shape[0]
    block = QUERY_FEATURES + 2 * KEY_FEATURES
    block = block // width
    inputs_f = x_ref[...].astype(F32)
    xn = (inputs_f * rms_scale(inputs_f) * gain_ref[...]).astype(BF16)
    for c in range(width):
        part = nn(xn, w_ref[c, :, :block])
        rows_scr[:, c * block : (c + 1) * block] = part.astype(BF16).astype(F32)
    half_rows = own_rows // 2
    turned = []
    for p in range(13):
        chunk = rows_scr[:, p * LANES : (p + 1) * LANES]
        if p < 10:
            chunk = turn(chunk, cos_ref[...], sin_ref[...])
        turned.append(chunk)
        for half in range(2):
            h = 2 * p + half
            if h < QUERY_HEADS:
                piece = chunk if half == 0 else swap_halves(chunk)
                piece = keep_low(piece.astype(BF16).astype(F32) * 0.125).astype(BF16)
                g, j = divmod(h, HEADS_PER_GROUP)
                for b in range(2):
                    q_ref[g, b, j * half_rows : (j + 1) * half_rows, :] = piece[
                        b * half_rows : (b + 1) * half_rows
                    ]
    for g in range(KEY_VALUE_HEADS):
        k_piece = QUERY_HEADS + g
        v_piece = QUERY_HEADS + KEY_VALUE_HEADS + g
        key = turned[k_piece // 2]
        key = key if k_piece % 2 == 0 else swap_halves(key)
        value = turned[v_piece // 2]
        value = value if v_piece % 2 == 1 else swap_halves(value)
        ids = lane_ids(own_rows)
        kv_ref[g] = jnp.where(ids < HEAD_DIMENSION, key, value).astype(BF16)


def project(x, gain, w_a, cosine, sine):
    own_rows, model_width = x.shape
    width = w_a.shape[0]
    q_shape = (KEY_VALUE_HEADS, 2, HEADS_PER_GROUP * own_rows // 2, LANES)
    kv_shape = (KEY_VALUE_HEADS, own_rows, LANES)
    return pl.pallas_call(
        project_kernel,
        grid=(1,),
        out_shape=(
            jax.ShapeDtypeStruct(q_shape, BF16),
            jax.ShapeDtypeStruct(kv_shape, BF16),
        ),
        in_specs=[
            full_spec(x.shape),
            full_spec(gain.shape),
            pl.BlockSpec((width, model_width, 512), lambda i: (0, 0, 0)),
            full_spec(cosine.shape),
            full_spec(sine.shape),
        ],
        out_specs=(full_spec(q_shape), full_spec(kv_shape)),
        scratch_shapes=[pltpu.VMEM((own_rows, 13 * LANES), F32)],
        compiler_params=pltpu.CompilerParams(vmem_limit_bytes=VMEM_BYTES),
        name="project",
    )(x, gain, w_a, cosine, sine)


def fill_bias(low_ref, start_ref, bias_scr):
    half_rows = bias_scr.shape[2]
    for b in range(2):
        starts = start_ref[b * half_rows : (b + 1) * half_rows, :]
        ids = lax.broadcasted_iota(jnp.int32, (half_rows, LANES), 1)
        own = lax.broadcasted_iota(jnp.int32, (half_rows, LANES), 0) + (
            LONGEST + b * half_rows
        )

        def one_tile(t, carry, b=b, starts=starts, ids=ids, own=own):
            for part in range(TILE // LANES):
                keys = ids + (t * TILE + part * LANES)
                allowed = (keys >= starts) & (keys <= own)
                bias_scr[b, t, :, part * LANES : (part + 1) * LANES] = jnp.where(
                    allowed, 0.0, NEG_FILL
                )
            return carry

        lax.fori_loop(low_ref[b], 5 + b, one_tile, 0)


def attend_kernel(low_ref, start_ref, q_ref, kv_ref, o_ref, logsum_ref, bias_scr, s_scr, m_scr, acc_scr):
    half_rows = bias_scr.shape[2]

    @pl.when(pl.program_id(0) == 0)
    def _():
        fill_bias(low_ref, start_ref, bias_scr)

    ones = jnp.ones((TILE, LANES), BF16)
    for b in range(2):
        low, high = low_ref[b], 5 + b
        m_scr[...] = jnp.full(m_scr.shape, -3e38, F32)

        def scores_of(t, carry, b=b):
            keys = kv_ref[0, pl.ds(pl.multiple_of(t * TILE, TILE), TILE), :]
            s = nt(q_ref[0, b], keys)
            bias = bias_scr[b, t]
            for j in range(HEADS_PER_GROUP):
                rows = slice(j * half_rows, (j + 1) * half_rows)
                part = s[rows] + bias
                s_scr[t, rows, :] = part
                m_scr[rows, :] = jnp.maximum(
                    m_scr[rows, :], jnp.maximum(part[:, :LANES], part[:, LANES:])
                )
            return carry

        lax.fori_loop(low, high, scores_of, 0)
        row_max = jnp.max(m_scr[...], axis=1, keepdims=True)
        acc_scr[...] = jnp.zeros_like(acc_scr)

        def weigh(t, carry, row_max=row_max):
            keys = kv_ref[0, pl.ds(pl.multiple_of(t * TILE, TILE), TILE), :]
            p = jnp.exp(s_scr[t] - row_max).astype(BF16)
            acc_scr[...] += nn(p, jnp.concatenate([keys, ones], axis=1))
            return carry

        lax.fori_loop(low, high, weigh, 0)
        total = acc_scr[:, LANES:]
        o_ref[0, b] = keep_high(acc_scr[:, :LANES] / total).astype(BF16)
        logsum_ref[0, b] = row_max + jnp.log(total)


def attend(low, start, q, kv):
    groups, blocks, rows, lanes = q.shape
    half_rows = rows // HEADS_PER_GROUP
    window = kv.shape[1]
    q_spec = pl.BlockSpec((1, blocks, rows, lanes), lambda g: (g, 0, 0, 0))
    return pl.pallas_call(
        attend_kernel,
        grid=(groups,),
        out_shape=(
            jax.ShapeDtypeStruct(q.shape, BF16),
            jax.ShapeDtypeStruct(q.shape, F32),
        ),
        in_specs=[
            pl.BlockSpec(memory_space=pltpu.SMEM),
            full_spec(start.shape),
            q_spec,
            pl.BlockSpec((1, window, lanes), lambda g: (g, 0, 0)),
        ],
        out_specs=(q_spec, q_spec),
        scratch_shapes=[
            pltpu.VMEM((2, window // TILE, half_rows, TILE), F32),
            pltpu.VMEM((window // TILE, rows, TILE), F32),
            pltpu.VMEM((rows, lanes), F32),
            pltpu.VMEM((rows, TILE), F32),
        ],
        compiler_params=pltpu.CompilerParams(vmem_limit_bytes=VMEM_BYTES),
        name="attend",
    )(low, start, q, kv)


def attend_back_kernel(
    low_ref, start_ref, q_ref, kv_ref, o_ref, do_ref, logsum_ref, dq_ref, dkv_ref, bias_scr, acc_scr, dq_scr
):
    half_rows = bias_scr.shape[2]

    @pl.when(pl.program_id(0) == 0)
    def _():
        fill_bias(low_ref, start_ref, bias_scr)

    acc_scr[...] = jnp.zeros_like(acc_scr)
    for b in range(2):
        low, high = low_ref[b], 5 + b
        delta = jnp.sum(
            o_ref[0, b].astype(F32) * do_ref[0, b].astype(F32), axis=1, keepdims=True
        )
        q_t = q_ref[0, b].T
        do_t = do_ref[0, b].T
        dq_scr[...] = jnp.zeros_like(dq_scr)

        def one_tile(t, carry, b=b, delta=delta, q_t=q_t, do_t=do_t):
            keys = kv_ref[0, pl.ds(pl.multiple_of(t * TILE, TILE), TILE), :]
            bias = bias_scr[b, t]
            s = nt(q_ref[0, b], keys)
            dp = nt(do_ref[0, b], keys)
            ds_parts, p_parts = [], []
            for j in range(HEADS_PER_GROUP):
                rows = slice(j * half_rows, (j + 1) * half_rows)
                sub = logsum_ref[0, b, rows, :]
                p = jnp.exp(s[rows] + bias - jnp.concatenate([sub, sub], axis=1))
                ds_parts.append((p * (dp[rows] - delta[rows])).astype(BF16))
                p_parts.append(p.astype(BF16))
            ds = jnp.concatenate(ds_parts, axis=0)
            p_low = jnp.concatenate(p_parts, axis=0)
            dq_scr[...] += nn(ds, keys)
            acc_scr[t] += nn(q_t, ds) + nn(do_t, p_low)
            return carry

        lax.fori_loop(low, high, one_tile, 0)
        dq_ref[0, b] = dq_scr[...]
    for t in range(acc_scr.shape[0]):
        dkv_ref[0, t * TILE : (t + 1) * TILE, :] = acc_scr[t].T.astype(BF16)


def attend_back(low, start, q, kv, o, do, logsum):
    groups, blocks, rows, lanes = q.shape
    half_rows = rows // HEADS_PER_GROUP
    window = kv.shape[1]
    q_spec = pl.BlockSpec((1, blocks, rows, lanes), lambda g: (g, 0, 0, 0))
    kv_spec = pl.BlockSpec((1, window, lanes), lambda g: (g, 0, 0))
    return pl.pallas_call(
        attend_back_kernel,
        grid=(groups,),
        out_shape=(
            jax.ShapeDtypeStruct(q.shape, F32),
            jax.ShapeDtypeStruct(kv.shape, BF16),
        ),
        in_specs=[
            pl.BlockSpec(memory_space=pltpu.SMEM),
            full_spec(start.shape),
            q_spec,
            kv_spec,
            q_spec,
            q_spec,
            q_spec,
        ],
        out_specs=(q_spec, kv_spec),
        scratch_shapes=[
            pltpu.VMEM((2, window // TILE, half_rows, TILE), F32),
            pltpu.VMEM((window // TILE, lanes, TILE), F32),
            pltpu.VMEM((rows, lanes), F32),
        ],
        compiler_params=pltpu.CompilerParams(vmem_limit_bytes=VMEM_BYTES),
        name="attend_back",
    )(low, start, q, kv, o, do, logsum)


def middle_kernel(
    x_ref,
    o_ref,
    cot_ref,
    gain_ref,
    wo_ref,
    w_ref,
    g_ref,
    out_ref,
    rg_ref,
    do_ref,
    go_ref,
    gain_grad_ref,
    attn_scr,
    wide_scr,
    xn_scr,
    xn_t_scr,
    cot_t_scr,
    res_scr,
    scale_scr,
    mlp_scr,
    xg_scr,
    hid_scr,
    gg_scr,
    ug_scr,
):
    step = pl.program_id(0)
    width = wo_ref.shape[0]
    own_rows = x_ref.shape[0]
    half_rows = own_rows // 2
    block = QUERY_FEATURES // width
    model_width = x_ref.shape[1]

    @pl.when(step == 0)
    def _():
        for p in range(8):
            for b in range(2):
                rows = slice(b * half_rows, (b + 1) * half_rows)
                g, j = divmod(2 * p, HEADS_PER_GROUP)
                pair = swap_halves(
                    o_ref[g, b, j * half_rows : (j + 1) * half_rows, :].astype(F32)
                )
                if 2 * p + 1 < QUERY_HEADS:
                    g, j = divmod(2 * p + 1, HEADS_PER_GROUP)
                    pair = pair + o_ref[
                        g, b, j * half_rows : (j + 1) * half_rows, :
                    ].astype(F32)
                attn_scr[rows, p * LANES : (p + 1) * LANES] = pair.astype(BF16)
        residual = x_ref[...].astype(F32)
        for c in range(width):
            residual = residual + nt(
                attn_scr[:, c * block : (c + 1) * block], wo_ref[c, :, :block]
            )
        scale = rms_scale(residual)
        scale_scr[...] = scale
        res_scr[...] = residual
        xn = (residual * scale * gain_ref[...]).astype(BF16)
        xn_scr[...] = xn
        xn_t_scr[...] = xn.T
        cot_t_scr[...] = cot_ref[...].T
        mlp_scr[...] = jnp.zeros_like(mlp_scr)
        xg_scr[...] = jnp.zeros_like(xg_scr)

    def one_part(i, carry):
        rows = pl.ds(pl.multiple_of(i * half_rows, half_rows), half_rows)
        xn = xn_scr[rows, :]
        gate = nn(xn, w_ref[0, 0])
        up = nn(xn, w_ref[0, 1])
        hid_grad = nn(cot_ref[rows, :], w_ref[0, 2])
        sig = 1.0 / (1.0 + jnp.exp(-gate))
        act = gate * sig
        hid = (act * up).astype(BF16)
        gg = (hid_grad * up * sig * (1.0 + gate * (1.0 - sig))).astype(BF16)
        ug = (hid_grad * act).astype(BF16)
        hid_scr[rows, :] = hid
        gg_scr[rows, :] = gg
        ug_scr[rows, :] = ug
        mlp_scr[rows, :] += nt(hid, w_ref[0, 2])
        xg_scr[rows, :] += nt(gg, w_ref[0, 0]) + nt(ug, w_ref[0, 1])
        return carry

    lax.fori_loop(0, 2, one_part, 0)

    part_rows = model_width // 4

    def one_grad(i, carry):
        rows = pl.ds(pl.multiple_of(i * part_rows, 16), part_rows)
        xn_t = xn_t_scr[rows, :]
        g_ref[0, 0, rows, :] = nn(xn_t, gg_scr[...]).astype(BF16)
        g_ref[0, 1, rows, :] = nn(xn_t, ug_scr[...]).astype(BF16)
        g_ref[0, 2, rows, :] = nn(cot_t_scr[rows, :], hid_scr[...]).astype(BF16)
        return carry

    lax.fori_loop(0, 4, one_grad, 0)

    @pl.when(step == pl.num_programs(0) - 1)
    def _():
        residual = res_scr[...]
        scale = scale_scr[...]
        out_ref[...] = (residual + mlp_scr[...]).astype(BF16)
        normed = residual * scale
        xg = xg_scr[...]
        gain_grad_ref[...] = jnp.sum(xg * normed, axis=0, keepdims=True)
        e = xg * gain_ref[...]
        rg = cot_ref[...].astype(F32) + scale * (
            e - normed * jnp.mean(e * normed, axis=1, keepdims=True)
        )
        rg_ref[...] = rg
        branch = rg.astype(BF16)
        branch_t = branch.T
        for c in range(width):
            wide_scr[:, c * block : (c + 1) * block] = (
                nn(branch, wo_ref[c, :, :block]).astype(BF16).astype(F32)
            )
            go_ref[c, :, :block] = nn(
                branch_t, attn_scr[:, c * block : (c + 1) * block]
            ).astype(BF16)
            go_ref[c, :, block:] = jnp.zeros((model_width, go_ref.shape[2] - block), BF16)
        for h in range(QUERY_HEADS):
            g, j = divmod(h, HEADS_PER_GROUP)
            p, half = divmod(h, 2)
            piece = wide_scr[:, p * LANES : (p + 1) * LANES]
            piece = keep_high(piece if half == 1 else swap_halves(piece)).astype(BF16)
            for b in range(2):
                do_ref[g, b, j * half_rows : (j + 1) * half_rows, :] = piece[
                    b * half_rows : (b + 1) * half_rows
                ]


def middle(x, o, cot, gain, w_a, w_b):
    own_rows, model_width = x.shape
    width, kinds, _, block = w_b.shape
    row_spec = full_spec(x.shape)
    rows_f32 = pltpu.VMEM((own_rows, model_width), F32)
    w_spec = pl.BlockSpec((1, kinds, model_width, block), lambda c: (c, 0, 0, 0))
    return pl.pallas_call(
        middle_kernel,
        grid=(width,),
        out_shape=(
            jax.ShapeDtypeStruct(w_b.shape, BF16),
            jax.ShapeDtypeStruct(x.shape, BF16),
            jax.ShapeDtypeStruct(x.shape, F32),
            jax.ShapeDtypeStruct(o.shape, BF16),
            jax.ShapeDtypeStruct((width, model_width, TILE), BF16),
            jax.ShapeDtypeStruct((1, model_width), F32),
        ),
        in_specs=[
            row_spec,
            full_spec(o.shape),
            row_spec,
            full_spec(gain.shape),
            pl.BlockSpec((width, model_width, TILE), lambda c: (0, 0, 2)),
            w_spec,
        ],
        out_specs=(
            w_spec,
            row_spec,
            row_spec,
            full_spec(o.shape),
            full_spec((width, model_width, TILE)),
            full_spec((1, model_width)),
        ),
        scratch_shapes=[
            pltpu.VMEM((own_rows, 1024), BF16),
            pltpu.VMEM((own_rows, 1024), F32),
            pltpu.VMEM((own_rows, model_width), BF16),
            pltpu.VMEM((model_width, own_rows), BF16),
            pltpu.VMEM((model_width, own_rows), BF16),
            rows_f32,
            pltpu.VMEM((own_rows, 1), F32),
            rows_f32,
            rows_f32,
            pltpu.VMEM((own_rows, block), BF16),
            pltpu.VMEM((own_rows, block), BF16),
            pltpu.VMEM((own_rows, block), BF16),
        ],
        compiler_params=pltpu.CompilerParams(vmem_limit_bytes=VMEM_BYTES),
        name="middle",
    )(x, o, cot, gain, w_a, w_b)


def finish_kernel(
    x_ref, gain_ref, w_ref, cos_ref, sin_ref, dq_ref, dkv_ref, rg_ref, g_ref, out_ref, gain_grad_ref, wide_scr
):
    own_rows, model_width = x_ref.shape
    width = w_ref.shape[0]
    half_rows = own_rows // 2
    block = (QUERY_FEATURES + 2 * KEY_FEATURES) // width

    def low_piece(i):
        if i < QUERY_HEADS:
            g, j = divmod(i, HEADS_PER_GROUP)
            rows = slice(j * half_rows, (j + 1) * half_rows)
            whole = jnp.concatenate([dq_ref[g, 0, rows, :], dq_ref[g, 1, rows, :]], axis=0)
            return keep_low(whole * 0.125)
        g = (i - QUERY_HEADS) % KEY_VALUE_HEADS
        whole = (
            dkv_ref[g, 0].astype(F32) + dkv_ref[g, 1].astype(F32) + dkv_ref[g, 2].astype(F32)
        )
        if i < QUERY_HEADS + KEY_VALUE_HEADS:
            return keep_low(whole)
        return keep_low(swap_halves(whole))

    for p in range(13):
        chunk = low_piece(2 * p)
        if 2 * p + 1 < QUERY_HEADS + 2 * KEY_VALUE_HEADS:
            chunk = chunk + swap_halves(low_piece(2 * p + 1))
        if p < 10:
            chunk = turn(chunk, cos_ref[...], -sin_ref[...])
        wide_scr[:, p * LANES : (p + 1) * LANES] = chunk.astype(BF16)
    inputs_f = x_ref[...].astype(F32)
    scale = rms_scale(inputs_f)
    normed = inputs_f * scale
    xn_t = (normed * gain_ref[...]).astype(BF16).T
    xg = jnp.zeros((own_rows, model_width), F32)
    for c in range(width):
        part = wide_scr[:, c * block : (c + 1) * block]
        xg = xg + nt(part, w_ref[c, :, :block])
        g_ref[c, :, :block] = nn(xn_t, part).astype(BF16)
        g_ref[c, :, block:] = jnp.zeros((model_width, g_ref.shape[2] - block), BF16)
    gain_grad_ref[...] = jnp.sum(xg * normed, axis=0, keepdims=True)
    e = xg * gain_ref[...]
    out_ref[...] = (
        rg_ref[...] + scale * (e - normed * jnp.mean(e * normed, axis=1, keepdims=True))
    ).astype(BF16)


def finish(x, gain, w_a, cosine, sine, dq, dkv, rg):
    own_rows, model_width = x.shape
    width = w_a.shape[0]
    w_spec = pl.BlockSpec((width, model_width, 512), lambda i: (0, 0, 0))
    return pl.pallas_call(
        finish_kernel,
        grid=(1,),
        out_shape=(
            jax.ShapeDtypeStruct((width, model_width, 512), BF16),
            jax.ShapeDtypeStruct(x.shape, BF16),
            jax.ShapeDtypeStruct((1, model_width), F32),
        ),
        in_specs=[
            full_spec(x.shape),
            full_spec(gain.shape),
            w_spec,
            full_spec(cosine.shape),
            full_spec(sine.shape),
            full_spec(dq.shape),
            full_spec(dkv.shape),
            full_spec(rg.shape),
        ],
        out_specs=(
            w_spec,
            full_spec(x.shape),
            full_spec((1, model_width)),
        ),
        scratch_shapes=[pltpu.VMEM((own_rows, 13 * LANES), BF16)],
        compiler_params=pltpu.CompilerParams(vmem_limit_bytes=VMEM_BYTES),
        name="finish",
    )(x, gain, w_a, cosine, sine, dq, dkv, rg)


def rotation_tables(position):
    half = HEAD_DIMENSION // 2
    lanes = jnp.arange(LANES, dtype=jnp.int32)
    inverse = jnp.exp((lanes % half).astype(F32) * (-2.0 * math.log(THETA) / HEAD_DIMENSION))
    sign = jnp.where(lanes % HEAD_DIMENSION < half, -1.0, 1.0)
    angles = position.astype(F32)[:, None] * inverse[None, :]
    return jnp.cos(angles), jnp.sin(angles) * sign[None, :]


MESH = pl.DeviceIdType.MESH
ANY_SPEC = pl.BlockSpec(memory_space=pl.ANY)


def remote(src, dst, send_sem, recv_sem, device):
    return pltpu.make_async_remote_copy(
        src_ref=src,
        dst_ref=dst,
        send_sem=send_sem,
        recv_sem=recv_sem,
        device_id=device,
        device_id_type=MESH,
    )


def loop(count, body):
    def step(i, carry):
        body(i)
        return carry

    lax.fori_loop(0, count, step, 0)


def signal(device):
    pl.semaphore_signal(
        pltpu.get_barrier_semaphore(), inc=1, device_id=device, device_id_type=MESH
    )


class Place:
    def __init__(self, n_row, n_col):
        self.n_row, self.n_col, self.n_z = n_row, n_col, n_row // 2
        self.row, self.col = lax.axis_index("row"), lax.axis_index("col")
        self.z, self.x = self.row // 2, lax.rem(self.row, 2)
        self.y, self.k = self.col // 2, lax.rem(self.col, 2)
        self.second = self.x + self.k * (self.y - self.x)
        self.third = self.y + self.k * (self.x - self.y)
        self.partner = (self.row, 2 * self.y + (1 - self.k))
        self.by_second = self.device(self.z, 1 - self.second, self.third)
        self.by_third = self.device(self.z, self.second, 1 - self.third)

    def xy(self, second, third):
        return second + self.k * (third - second), third + self.k * (second - third)

    def device(self, z, second, third):
        x, y = self.xy(second, third)
        return (2 * z + x, 2 * y + self.k)

    def along_z(self, z):
        return (2 * z + self.x, self.col)

    def greet(self, with_cols):
        row, col, n_row, n_col = self.row, self.col, self.n_row, self.n_col
        loop(n_row - 1, lambda i: signal((lax.rem(row + 1 + i, n_row), col)))
        if with_cols:
            loop(n_col - 1, lambda i: signal((row, lax.rem(col + 1 + i, n_col))))
            count = n_col - 1
        else:
            signal(self.partner)
            signal((row, lax.rem(col + 2, 4)))
            count = 2
        pl.semaphore_wait(pltpu.get_barrier_semaphore(), n_row - 1 + count)


def slot(ref, kind, col, row, rows):
    if len(ref.shape) == 5:
        return ref.at[col, kind, row]
    return ref.at[col, kind, pl.ds(pl.multiple_of(row * rows, 8), rows), :]


def spread_shape(n_row, n_col, kinds, rows, columns):
    if rows % 8:
        return (n_col, kinds, n_row, rows, columns)
    return (n_col, kinds, n_row * rows, columns)


def deal_copies(me, src, dst, send_sems, recv_sems, i):
    block = src.shape[0] // me.n_row
    peer = lax.rem(me.row + 1 + i, me.n_row)
    giver = lax.rem(me.row + 2 * me.n_row - 1 - i, me.n_row)

    def rows(r):
        return pl.ds(pl.multiple_of(r * block, 8), block)

    out = remote(
        src.at[rows(peer), :], dst.at[rows(me.row), :], send_sems.at[i], recv_sems.at[i], (peer, me.col)
    )
    arrival = remote(
        src.at[rows(peer), :], dst.at[rows(giver), :], send_sems.at[i], recv_sems.at[i], (peer, me.col)
    )
    return out, arrival


def own_block(me, src, dst, sem):
    block = src.shape[0] // me.n_row
    rows = pl.ds(pl.multiple_of(me.row * block, 8), block)
    return pltpu.make_async_copy(src.at[rows, :], dst.at[rows, :], sem)


def gather_kernel(
    n_row,
    n_col,
    x_in,
    cot_in,
    a_in,
    b_in,
    x_out,
    cot_out,
    a_out,
    b_out,
    local_sems,
    deal_send,
    deal_recv,
    z_send,
    z_recv,
    own_send,
    s2_send,
    s2_recv,
    s3_send,
    s3_recv,
    p_send,
    p_recv,
):
    me = Place(n_row, n_col)
    n_z = me.n_z
    rows = a_in.shape[1]
    chunks = [(a_in, a_out, 0)] + [(b_in, b_out, kind) for kind in range(b_in.shape[0])]
    count = len(chunks)

    def at(q, z, second, third, k):
        _, dst, kind = chunks[q]
        x, y = me.xy(second, third)
        return slot(dst, kind, 2 * y + k, 2 * z + x, rows)

    def own(q):
        src, _, kind = chunks[q]
        return src.at[kind]

    def to_z(q, i):
        peer = lax.rem(me.z + 1 + i, n_z)
        return remote(
            own(q), at(q, me.z, me.second, me.third, me.k), z_send.at[q, i], z_recv.at[q, i], me.along_z(peer)
        )

    def from_z(q, i):
        giver = lax.rem(me.z + 2 * n_z - 1 - i, n_z)
        return giver, remote(
            own(q), at(q, giver, me.second, me.third, me.k), z_send.at[q, i], z_recv.at[q, i], me.along_z(giver)
        )

    def to_second(q, z, src):
        return remote(
            src, at(q, z, me.second, me.third, me.k), s2_send.at[q, z], s2_recv.at[q, z], me.by_second
        )

    def to_third(q, z, second, src):
        return remote(
            src, at(q, z, second, me.third, me.k), s3_send.at[q, second, z], s3_recv.at[q, second, z], me.by_third
        )

    def to_partner(q, z, second, third, src):
        x, y = me.xy(second, third)
        index = 2 * x + y
        return remote(
            src, at(q, z, second, third, me.k), p_send.at[q, index, z], p_recv.at[q, index, z], me.partner
        )

    me.greet(False)
    locals_ = [own_block(me, x_in, x_out, local_sems.at[0]), own_block(me, cot_in, cot_out, local_sems.at[1])]
    for q in range(count):
        locals_.append(
            pltpu.make_async_copy(own(q), at(q, me.z, me.second, me.third, me.k), local_sems.at[2 + q])
        )
    for copy in locals_:
        copy.start()

    def begin(q):
        loop(n_z - 1, lambda i: to_z(q, i).start())
        to_second(q, me.z, own(q)).start()
        to_third(q, me.z, me.second, own(q)).start()
        to_partner(q, me.z, me.second, me.third, own(q)).start()

    def deal(src, dst, index):
        loop(n_row - 1, lambda i: deal_copies(me, src, dst, deal_send.at[index], deal_recv.at[index], i)[0].start())

    deal(x_in, x_out, 0)
    for q in range(count):
        begin(q)
    deal(cot_in, cot_out, 1)

    def pass_z(q):
        def one(i):
            giver, arrival = from_z(q, i)
            arrival.wait_recv()
            src = at(q, giver, me.second, me.third, me.k)
            to_second(q, giver, src).start()
            to_third(q, giver, me.second, src).start()
            to_partner(q, giver, me.second, me.third, src).start()

        loop(n_z - 1, one)

    def pass_second(q):
        def one(z):
            src = at(q, z, 1 - me.second, me.third, me.k)
            remote(src, src, s2_send.at[q, z], s2_recv.at[q, z], me.by_second).wait_recv()
            to_third(q, z, 1 - me.second, src).start()
            to_partner(q, z, 1 - me.second, me.third, src).start()

        loop(n_z, one)

    def pass_third(q):
        def one(i):
            second, z = i // n_z, lax.rem(i, n_z)
            src = at(q, z, second, 1 - me.third, me.k)
            remote(
                src, src, s3_send.at[q, second, z], s3_recv.at[q, second, z], me.by_third
            ).wait_recv()
            to_partner(q, z, second, 1 - me.third, src).start()

        loop(2 * n_z, one)

    for t in range(count + 2):
        if t < count:
            pass_z(t)
        if 0 <= t - 1 < count:
            pass_second(t - 1)
        if 0 <= t - 2 < count:
            pass_third(t - 2)

    for q in range(count):

        def from_partner(i, q=q):
            index, z = i // n_z, lax.rem(i, n_z)
            _, dst, kind = chunks[q]
            src = slot(dst, kind, 2 * lax.rem(index, 2) + 1 - me.k, 2 * z + index // 2, rows)
            copy = remote(src, src, p_send.at[q, index, z], p_recv.at[q, index, z], me.partner)
            copy.wait_recv()
            copy.wait_send()

        loop(4 * n_z, from_partner)
        loop(n_z - 1, lambda i, q=q: to_z(q, i).wait_send())
        loop(n_z, lambda z, q=q: to_second(q, z, own(q)).wait_send())
        loop(2 * n_z, lambda i, q=q: to_third(q, lax.rem(i, n_z), i // n_z, own(q)).wait_send())
    for index, (src, dst) in enumerate(((x_in, x_out), (cot_in, cot_out))):

        def finish_deal(i, index=index, src=src, dst=dst):
            out, arrival = deal_copies(me, src, dst, deal_send.at[index], deal_recv.at[index], i)
            out.wait_send()
            arrival.wait_recv()

        loop(n_row - 1, finish_deal)
    for copy in locals_:
        copy.wait()


def gather_all(n_row, n_col, x, cot, pack_a, pack_b):
    n_z = n_row // 2
    rows = pack_a.shape[1]
    count = 1 + pack_b.shape[0]
    dma = pltpu.SemaphoreType.DMA
    a_shape = spread_shape(n_row, n_col, 1, rows, pack_a.shape[2])
    b_shape = spread_shape(n_row, n_col, pack_b.shape[0], rows, pack_b.shape[2])
    x, cot, w_a, w_b = pl.pallas_call(
        functools.partial(gather_kernel, n_row, n_col),
        out_shape=(
            jax.ShapeDtypeStruct(x.shape, BF16),
            jax.ShapeDtypeStruct(cot.shape, BF16),
            jax.ShapeDtypeStruct(a_shape, BF16),
            jax.ShapeDtypeStruct(b_shape, BF16),
        ),
        in_specs=[ANY_SPEC] * 4,
        out_specs=(ANY_SPEC,) * 4,
        scratch_shapes=[
            dma((2 + count,)),
            dma((2, n_row - 1)),
            dma((2, n_row - 1)),
            dma((count, n_z)),
            dma((count, n_z)),
            dma((count,)),
            dma((count, n_z)),
            dma((count, n_z)),
            dma((count, 2, n_z)),
            dma((count, 2, n_z)),
            dma((count, 4, n_z)),
            dma((count, 4, n_z)),
        ],
        compiler_params=pltpu.CompilerParams(collective_id=0, has_side_effects=True),
        name="gather_all",
    )(x, cot, pack_a, pack_b)
    model_width = n_row * rows
    w_a = w_a.reshape(n_col, model_width, pack_a.shape[2])
    w_b = w_b.reshape(n_col, pack_b.shape[0], model_width, pack_b.shape[2])
    return x, cot, w_a, w_b


def window_kernel(kv_in, kv_out, local_sem, send_a, recv_a, send_b, recv_b):
    row, col = lax.axis_index("row"), lax.axis_index("col")
    groups = kv_in.shape[0]

    def far(g, src, device):
        return remote(src, kv_out.at[g, 0], send_a.at[g], recv_a.at[g], device)

    def near(g, src, device):
        return remote(src, kv_out.at[g, 1], send_b.at[g], recv_b.at[g], device)

    for other in range(1, 4):
        signal((row, lax.rem(col + other, 4)))
    pl.semaphore_wait(pltpu.get_barrier_semaphore(), 3)
    local = pltpu.make_async_copy(kv_in, kv_out.at[:, 2], local_sem)
    local.start()

    @pl.when(col < 2)
    def _():
        loop(groups, lambda g: far(g, kv_in.at[g], (row, col + 2)).start())

    @pl.when(lax.rem(col, 2) == 0)
    def _():
        loop(groups, lambda g: near(g, kv_in.at[g], (row, col + 1)).start())

    @pl.when(col == 2)
    def _():
        def one(g):
            far(g, kv_in.at[g], (row, 0)).wait_recv()
            near(g, kv_in.at[g], (row, 3)).wait()

        loop(groups, one)

    @pl.when(col == 3)
    def _():
        def one(g):
            far(g, kv_in.at[g], (row, 1)).wait_recv()
            near(g, kv_out.at[g, 0], (row, 2)).start()

        def two(g):
            near(g, kv_out.at[g, 0], (row, 2)).wait()

        loop(groups, one)
        loop(groups, two)

    @pl.when(col == 1)
    def _():
        loop(groups, lambda g: near(g, kv_in.at[g], (row, 0)).wait_recv())

    @pl.when(col == 0)
    def _():
        loop(groups, lambda g: near(g, kv_in.at[g], (row, 1)).wait_send())

    @pl.when(col < 2)
    def _():
        loop(groups, lambda g: far(g, kv_in.at[g], (row, col + 2)).wait_send())

    local.wait()


def key_window(kv):
    groups, own_rows, lanes = kv.shape
    dma = pltpu.SemaphoreType.DMA
    out = pl.pallas_call(
        window_kernel,
        out_shape=jax.ShapeDtypeStruct((groups, 3, own_rows, lanes), BF16),
        in_specs=[ANY_SPEC],
        out_specs=ANY_SPEC,
        scratch_shapes=[dma, dma((groups,)), dma((groups,)), dma((groups,)), dma((groups,))],
        compiler_params=pltpu.CompilerParams(collective_id=1, has_side_effects=True),
        name="key_window",
    )(kv)
    return out.reshape(groups, 3 * own_rows, lanes)


def return_kernel(dkv_in, dkv_out, mail, local_sem, send_a, recv_a, send_b, recv_b):
    row, col = lax.axis_index("row"), lax.axis_index("col")
    groups = dkv_in.shape[0]

    def far(g, src, device):
        return remote(src, dkv_out.at[g, 2], send_a.at[g], recv_a.at[g], device)

    def near(g, device):
        return remote(dkv_in.at[g, 1], dkv_out.at[g, 1], send_b.at[g], recv_b.at[g], device)

    def aside(g):
        return remote(dkv_in.at[g, 1], mail.at[g], send_b.at[g], recv_b.at[g], (row, 3))

    for other in range(1, 4):
        signal((row, lax.rem(col + other, 4)))
    pl.semaphore_wait(pltpu.get_barrier_semaphore(), 3)
    for g in range(groups):
        dkv_out[g, 0] = dkv_in[g, 2]

    @pl.when(col == 2)
    def _():
        def one(g):
            aside(g).start()
            far(g, dkv_in.at[g, 0], (row, 0)).start()

        loop(groups, one)

    @pl.when(col == 3)
    def _():
        loop(groups, lambda g: near(g, (row, 2)).start())

        def one(g):
            aside(g).wait_recv()
            mail[g] = (mail[g].astype(F32) + dkv_in[g, 0].astype(F32)).astype(BF16)
            far(g, mail.at[g], (row, 1)).start()

        loop(groups, one)

    @pl.when(col == 1)
    def _():
        loop(groups, lambda g: near(g, (row, 0)).start())

    @pl.when(lax.rem(col, 2) == 1)
    def _():
        for g in range(groups):
            dkv_out[g, 1] = jnp.zeros(dkv_out.shape[2:], BF16)

    @pl.when(col >= 2)
    def _():
        for g in range(groups):
            dkv_out[g, 2] = jnp.zeros(dkv_out.shape[2:], BF16)

    @pl.when(col < 2)
    def _():
        loop(groups, lambda g: far(g, mail.at[g], (row, col + 2)).wait_recv())

    @pl.when(col == 0)
    def _():
        loop(groups, lambda g: near(g, (row, 1)).wait_recv())

    @pl.when(col == 1)
    def _():
        loop(groups, lambda g: near(g, (row, 0)).wait_send())

    @pl.when(col == 2)
    def _():
        def one(g):
            near(g, (row, 3)).wait_recv()
            aside(g).wait_send()
            far(g, dkv_in.at[g, 0], (row, 0)).wait_send()

        loop(groups, one)

    @pl.when(col == 3)
    def _():
        def one(g):
            near(g, (row, 2)).wait_send()
            far(g, mail.at[g], (row, 1)).wait_send()

        loop(groups, one)


def return_keys(dkv):
    groups, window, lanes = dkv.shape
    own_rows = window // 3
    dma = pltpu.SemaphoreType.DMA
    vmem = pl.BlockSpec(memory_space=pltpu.VMEM)
    return pl.pallas_call(
        return_kernel,
        out_shape=jax.ShapeDtypeStruct((groups, 3, own_rows, lanes), BF16),
        in_specs=[vmem],
        out_specs=vmem,
        scratch_shapes=[
            pltpu.VMEM((groups, own_rows, lanes), BF16),
            dma,
            dma((groups,)),
            dma((groups,)),
            dma((groups,)),
            dma((groups,)),
        ],
        compiler_params=pltpu.CompilerParams(
            collective_id=2, has_side_effects=True, vmem_limit_bytes=VMEM_BYTES
        ),
        name="return_keys",
    )(dkv.reshape(groups, 3, own_rows, lanes))


class Stage:
    pass


def reduce_kernel(n_row, n_col, rows, layer_in, grad_in, gain_in, *refs):
    me = Place(n_row, n_col)
    n_z = me.n_z
    n_chunk = 5
    parts, refs = refs[:3], refs[3:]
    (layer_out, grad_out, gain_out, o_q, o_o, o_b), refs = refs[:6], refs[6:]
    (
        own_scr,
        ra_scr,
        rb_scr,
        rc_scr,
        rd_scr,
        gain_scr,
        gain_sum,
    ), refs = refs[:7], refs[7:]
    (
        local_sems,
        deal_send,
        deal_recv,
        col_send,
        col_recv,
        row_send,
        row_recv,
        load_sems,
        a_send,
        a_recv,
        b_send,
        b_recv,
        c_send,
        c_recv,
        d_send,
        d_recv,
    ) = refs
    g_q, g_o, g_b = parts
    chunks = [
        (g_b, 2, 640, lambda v: o_b.__setitem__(2, v)),
        (g_b, 0, 640, lambda v: o_b.__setitem__(0, v)),
        (g_b, 1, 640, lambda v: o_b.__setitem__(1, v)),
        (g_o, 0, 256, lambda v: o_o.__setitem__(0, v)),
        (g_q, 0, 512, lambda v: o_q.__setitem__(0, v)),
    ]

    def view(scr, q, *index):
        return scr.at[(q, *index, slice(None), pl.ds(0, chunks[q][2]))]

    def index_of(second, third):
        x, y = me.xy(second, third)
        return 2 * x + y

    def grad_at(q, xy, z, k):
        ref, kind, _, _ = chunks[q]
        return slot(ref, kind, 2 * lax.rem(xy, 2) + k, 2 * z + xy // 2, rows)

    def load(q, xy, z):
        return pltpu.make_async_copy(
            grad_at(q, xy, z, me.k), view(own_scr, q, xy, z), load_sems.at[q, xy, z]
        )

    def give(q, xy, z):
        return remote(
            grad_at(q, xy, z, 1 - me.k),
            view(ra_scr, q, xy, z),
            a_send.at[q, xy, z],
            a_recv.at[q, xy, z],
            me.partner,
        )

    def to_third(q, second, z):
        return remote(
            view(own_scr, q, index_of(second, 1 - me.third), z),
            view(rb_scr, q, second, z),
            b_send.at[q, second, z],
            b_recv.at[q, second, z],
            me.by_third,
        )

    def to_second(q, z):
        return remote(
            view(own_scr, q, index_of(1 - me.second, me.third), z),
            view(rc_scr, q, z),
            c_send.at[q, z],
            c_recv.at[q, z],
            me.by_second,
        )

    def to_z(q, i):
        peer = lax.rem(me.z + 1 + i, n_z)
        return remote(
            view(own_scr, q, index_of(me.second, me.third), peer),
            view(rd_scr, q, i),
            d_send.at[q, i],
            d_recv.at[q, i],
            me.along_z(peer),
        )

    def add(q, xy, z, other):
        mine = view(own_scr, q, xy, z)
        mine[...] = (mine[...].astype(F32) + other[...].astype(F32)).astype(BF16)

    def take_partner(q, xy, z):
        load(q, xy, z).wait()
        give(q, xy, z).wait_recv()
        add(q, xy, z, view(ra_scr, q, xy, z))

    def stage_b(q):
        def send(i):
            second = (1 - me.second) + (i // n_z) * (2 * me.second - 1)
            z = lax.rem(i, n_z)
            take_partner(q, index_of(second, 1 - me.third), z)
            to_third(q, second, z).start()

        loop(2 * n_z, send)

        def keep(i):
            second = (1 - me.second) + (i // n_z) * (2 * me.second - 1)
            take_partner(q, index_of(second, me.third), lax.rem(i, n_z))

        loop(2 * n_z, keep)

    def stage_c(q):
        def one(i):
            second = (1 - me.second) + (i // n_z) * (2 * me.second - 1)
            z = lax.rem(i, n_z)
            to_third(q, second, z).wait_recv()
            add(q, index_of(second, me.third), z, view(rb_scr, q, second, z))

        loop(n_z, lambda z: (one(z), to_second(q, z).start()))
        loop(n_z, lambda z: one(z + n_z))

    def stage_d(q):
        mine = index_of(me.second, me.third)

        def one(i):
            peer = lax.rem(me.z + 1 + i, n_z)
            to_second(q, peer).wait_recv()
            add(q, mine, peer, view(rc_scr, q, peer))

        loop(n_z - 1, lambda i: (one(i), to_z(q, i).start()))
        one(n_z - 1)

    def stage_e(q):
        mine = view(own_scr, q, index_of(me.second, me.third), me.z)
        loop(n_z - 1, lambda i: to_z(q, i).wait_recv())
        total = mine[...].astype(F32)
        for i in range(n_z - 1):
            total = total + view(rd_scr, q, i)[...].astype(F32)
        chunks[q][3](total)

    me.greet(True)
    locals_ = [
        own_block(me, layer_in, layer_out, local_sems.at[0]),
        own_block(me, grad_in, grad_out, local_sems.at[1]),
    ]
    for copy in locals_:
        copy.start()

    def col_copy(i):
        peer = lax.rem(me.col + 1 + i, n_col)
        return remote(
            gain_in, gain_scr.at[me.col], col_send.at[i], col_recv.at[i], (me.row, peer)
        )

    def row_copy(i):
        peer = lax.rem(me.row + 1 + i, n_row)
        return remote(
            gain_sum, gain_scr.at[n_col + me.row], row_send.at[i], row_recv.at[i], (peer, me.col)
        )

    loop(n_col - 1, lambda i: col_copy(i).start())
    for q in range(n_chunk):

        def begin(i, q=q):
            second = (1 - me.second) + lax.rem(i // n_z, 2) * (2 * me.second - 1)
            third = (1 - me.third) + (i // (2 * n_z)) * (2 * me.third - 1)
            z = lax.rem(i, n_z)
            load(q, index_of(second, third), z).start()
            give(q, i // n_z, z).start()

        loop(4 * n_z, begin)
    for index, (src, dst) in enumerate(((layer_in, layer_out), (grad_in, grad_out))):
        loop(
            n_row - 1,
            lambda i, src=src, dst=dst, index=index: deal_copies(
                me, src, dst, deal_send.at[index], deal_recv.at[index], i
            )[0].start(),
        )
    gain_scr[me.col] = gain_in[...]
    loop(n_col - 1, lambda i: col_copy(i).wait_recv())
    total = gain_scr[0]
    for c in range(1, n_col):
        total = total + gain_scr[c]
    gain_sum[...] = total
    gain_scr[n_col + me.row] = total
    loop(n_row - 1, lambda i: row_copy(i).start())

    for t in range(n_chunk + 3):
        if t < n_chunk:
            stage_b(t)
        if 0 <= t - 1 < n_chunk:
            stage_c(t - 1)
        if 0 <= t - 2 < n_chunk:
            stage_d(t - 2)
        if 0 <= t - 3 < n_chunk:
            stage_e(t - 3)

    loop(n_row - 1, lambda i: row_copy(i).wait_recv())
    total = gain_scr[n_col]
    for r in range(1, n_row):
        total = total + gain_scr[n_col + r]
    gain_out[...] = total

    loop(n_col - 1, lambda i: col_copy(i).wait_send())
    loop(n_row - 1, lambda i: row_copy(i).wait_send())
    for q in range(n_chunk):
        loop(4 * n_z, lambda i, q=q: give(q, i // n_z, lax.rem(i, n_z)).wait_send())
        loop(2 * n_z, lambda i, q=q: to_third(q, i // n_z, lax.rem(i, n_z)).wait_send())
        loop(n_z, lambda z, q=q: to_second(q, z).wait_send())
        loop(n_z - 1, lambda i, q=q: to_z(q, i).wait_send())
    for index, (src, dst) in enumerate(((layer_in, layer_out), (grad_in, grad_out))):

        def finish_deal(i, index=index, src=src, dst=dst):
            out, arrival = deal_copies(me, src, dst, deal_send.at[index], deal_recv.at[index], i)
            out.wait_send()
            arrival.wait_recv()

        loop(n_row - 1, finish_deal)
    for copy in locals_:
        copy.wait()


def reduce_all(n_row, n_col, layer_out, grad_in, gains, g_q, g_o, g_b):
    n_z = n_row // 2
    rows = g_b.shape[2] // n_row
    dma = pltpu.SemaphoreType.DMA
    vmem = pl.BlockSpec(memory_space=pltpu.VMEM)
    n_chunk = 5

    def shaped(values, kinds):
        return values.reshape(spread_shape(n_row, n_col, kinds, rows, values.shape[-1]))

    return pl.pallas_call(
        functools.partial(reduce_kernel, n_row, n_col, rows),
        out_shape=(
            jax.ShapeDtypeStruct(layer_out.shape, BF16),
            jax.ShapeDtypeStruct(grad_in.shape, BF16),
            jax.ShapeDtypeStruct(gains.shape, F32),
            jax.ShapeDtypeStruct((1, rows, g_q.shape[-1]), F32),
            jax.ShapeDtypeStruct((1, rows, g_o.shape[-1]), F32),
            jax.ShapeDtypeStruct((3, rows, g_b.shape[-1]), F32),
        ),
        in_specs=[ANY_SPEC, ANY_SPEC, vmem, ANY_SPEC, ANY_SPEC, ANY_SPEC],
        out_specs=(ANY_SPEC, ANY_SPEC, vmem, vmem, vmem, vmem),
        scratch_shapes=[
            pltpu.VMEM((n_chunk, 4, n_z, rows, 640), BF16),
            pltpu.VMEM((n_chunk, 4, n_z, rows, 640), BF16),
            pltpu.VMEM((n_chunk, 2, n_z, rows, 640), BF16),
            pltpu.VMEM((n_chunk, n_z, rows, 640), BF16),
            pltpu.VMEM((n_chunk, n_z - 1, rows, 640), BF16),
            pltpu.VMEM((n_col + n_row, *gains.shape), F32),
            pltpu.VMEM(gains.shape, F32),
            dma((2,)),
            dma((2, n_row - 1)),
            dma((2, n_row - 1)),
            dma((n_col - 1,)),
            dma((n_col - 1,)),
            dma((n_row - 1,)),
            dma((n_row - 1,)),
            dma((n_chunk, 4, n_z)),
            dma((n_chunk, 4, n_z)),
            dma((n_chunk, 4, n_z)),
            dma((n_chunk, 2, n_z)),
            dma((n_chunk, 2, n_z)),
            dma((n_chunk, n_z)),
            dma((n_chunk, n_z)),
            dma((n_chunk, n_z)),
            dma((n_chunk, n_z)),
        ],
        compiler_params=pltpu.CompilerParams(
            collective_id=3, has_side_effects=True, vmem_limit_bytes=VMEM_BYTES
        ),
        name="reduce_all",
    )(layer_out, grad_in, gains, shaped(g_q, 1), shaped(g_o, 1), shaped(g_b, 3))


def on_device(
    layer_input,
    norm1_gain,
    w_qkv,
    w_out,
    norm2_gain,
    w_gate,
    w_up,
    w_down,
    out_cotangent,
    seq_lengths,
    position_ids,
    deal_rows,
):
    own_rows, model_width = layer_input.shape
    n_row = lax.axis_size("row")
    n_col = lax.axis_size("col")
    block_rows = own_rows // n_row
    row_ids = jnp.arange(n_row, dtype=jnp.int32)
    targets = deal_rows[0]
    sender = jnp.sum(jnp.where(targets[:, None] == row_ids[None, :], row_ids[:, None], 0), axis=0)

    def pick(values, order):
        blocks = values.reshape(n_row, block_rows, model_width)
        return jnp.take(blocks, order, axis=0).reshape(own_rows, model_width)

    def pad(values, columns):
        return jnp.pad(values, ((0, 0), (0, columns - values.shape[1])))

    pack_a = jnp.concatenate([pad(w_qkv, 512), pad(w_out, 256)], axis=1)[None]
    pack_b = jnp.stack([w_gate, w_up, w_down])
    x, cot, w_a, w_b = gather_all(
        n_row, n_col, pick(layer_input, sender), pick(out_cotangent, sender), pack_a, pack_b
    )

    gain_one, gain_two = norm1_gain[None, :], norm2_gain[None, :]
    cosine, sine = rotation_tables(position_ids)
    col = lax.axis_index("col")
    bounds = jnp.cumsum(seq_lengths[0])
    own_ids = col * own_rows + jnp.arange(own_rows, dtype=jnp.int32)
    start = jnp.sum(
        jnp.where(own_ids[:, None] >= bounds[None, :], seq_lengths[0][None, :], 0), axis=1
    )
    start = start - (col * own_rows - LONGEST)
    low = jnp.stack([start[0], start[own_rows // 2]]) // TILE
    start = jnp.broadcast_to(start[:, None], (own_rows, LANES)).astype(jnp.int32)

    q, kv_own = project(x, gain_one, w_a, cosine, sine)
    kv = key_window(kv_own)
    o, logsum = attend(low, start, q, kv)
    g_b, layer_out, rg, do, g_o, gain_two_part = middle(x, o, cot, gain_two, w_a, w_b)
    dq, dkv = attend_back(low, start, q, kv, o, do, logsum)
    dkv = return_keys(dkv)
    g_q, grad_in, gain_one_part = finish(x, gain_one, w_a, cosine, sine, dq, dkv, rg)
    gains = jnp.concatenate([gain_one_part, gain_two_part], axis=0)
    gains = jnp.pad(gains, ((0, 6), (0, 1024 - model_width)))
    back_out, back_grad, gains, o_q, o_o, o_b = reduce_all(
        n_row, n_col, layer_out, grad_in, gains, g_q, g_o, g_b
    )
    return (
        pick(back_out, targets),
        pick(back_grad, targets),
        gains[0, :model_width],
        o_q[0, :, : w_qkv.shape[1]],
        o_o[0, :, : w_out.shape[1]],
        gains[1, :model_width],
        o_b[0],
        o_b[1],
        o_b[2],
    )


def solution(mesh):
    placed = (
        P(("row", "col"), None),
        P(),
        P("row", "col"),
        P("row", "col"),
        P(),
        P("row", "col"),
        P("row", "col"),
        P("row", "col"),
        P(("row", "col"), None),
        P("row", None),
        P(("row", "col")),
        P(("row", "col"), None),
    )
    return jax.shard_map(
        on_device,
        mesh=mesh,
        in_specs=placed,
        out_specs=(
            P(("row", "col"), None),
            P(("row", "col"), None),
            P(),
            P("row", "col"),
            P("row", "col"),
            P(),
            P("row", "col"),
            P("row", "col"),
            P("row", "col"),
        ),
        check_vma=False,
    )
```
